32 devices in a mesh: tm: 4 (over z), width: 4 (over x, core), head: 2 (over y).
Axes of the slice: x: 2, y: 2, z: 4, core: 2. Of those that a mesh axis runs over, the one named last changes fastest.
Arguments:
- query_heads: bfloat16 [12, 36, 40, 256], P('tm', None, 'width', 'head'), may hold values from -18 to 18
- key_heads: bfloat16 [12, 36, 40, 256], P('tm', None, 'width', 'head'), may hold values from -18 to 18
- value_heads: bfloat16 [12, 36, 40, 256], P('tm', None, 'width', 'head'), may hold values from -10 to 10
- row_valid: int32 [36], replicated, may hold values from 0 to 1, as said below
- out_weight: bfloat16 [256, 3072], P(None, 'head'), may hold values from -0.375 to 0.375
- grad_mixed: bfloat16 [12, 36, 40, 3072], P('tm', None, 'width', 'head'), may hold values from -6 to 6
Outputs:
- mixed: bfloat16 [12, 36, 40, 3072], P('tm', None, 'width', 'head')
- grad_query: bfloat16 [12, 36, 40, 256], P('tm', None, 'width', 'head')
- grad_key: bfloat16 [12, 36, 40, 256], P('tm', None, 'width', 'head')
- grad_value: bfloat16 [12, 36, 40, 256], P('tm', None, 'width', 'head')
- grad_weight: float32 [256, 3072], P(('tm', 'width'), 'head')
The draws below stay inside these ranges and needn't reach their ends.
Inputs may be any that keep to these rules, and one draw needn't show every extreme that they name: row_valid is 1 on every row before the last 9 rows; among the last 9 rows at least one is 1 and at least one is 0.
All inputs are finite; a program needn't handle non-finite values.
Results may differ from the reference program's by a relative error of at most 0.015.
Values may be sent and summed in bfloat16 or wider, within the bound.
A program may use at most 256 MiB of HBM per device.

```python
import math
import jax
import jax.numpy as jnp
from jax import lax

TF = 3
TH = 9
TW = 10
HD = 128
D = 3072
HEADS = 2
FRAMES = 12
ROWS = 36
COLS = 40
N_TM = 4
N_WIDTH = 4


def drawn_pair(key):
    full_shape = (FRAMES, ROWS, COLS, HEADS * HD)
    seeded = jax.random.fold_in(key, 11)
    query_array = jnp.clip(jax.random.normal(jax.random.fold_in(seeded, 1), full_shape, jnp.float32), -4.0, 4.0)
    key_array = jnp.clip(jax.random.normal(jax.random.fold_in(seeded, 2), full_shape, jnp.float32), -4.0, 4.0)
    return (query_array, key_array)


def draw_query_heads(key, part):
    return drawn_pair(key)[0].astype(jnp.bfloat16)


def draw_key_heads(key, part):
    return drawn_pair(key)[1].astype(jnp.bfloat16)


def draw_value_heads(key, part):
    full_shape = (FRAMES, ROWS, COLS, HEADS * HD)
    tile_shape = (FRAMES // TF, ROWS // TH, COLS // TW, HEADS * HD)
    seeded = jax.random.fold_in(key, 23)
    noise = jnp.clip(jax.random.normal(jax.random.fold_in(seeded, 1), full_shape, jnp.float32), -4.0, 4.0)
    offsets = jnp.clip(jax.random.normal(jax.random.fold_in(seeded, 2), tile_shape, jnp.float32), -3.0, 3.0)
    offsets = jnp.repeat(jnp.repeat(jnp.repeat(offsets, TF, axis=0), TH, axis=1), TW, axis=2)
    return (noise + 2.0 * offsets).astype(jnp.bfloat16)


def draw_row_valid(key, part):
    seeded = jax.random.fold_in(key, 31)
    bits = jax.random.randint(jax.random.fold_in(seeded, 1), (ROWS,), 0, 2)
    first = jax.random.randint(jax.random.fold_in(seeded, 2), (), 0, TH)
    second = (first + 1 + jax.random.randint(jax.random.fold_in(seeded, 3), (), 0, TH - 1)) % TH
    local = jnp.arange(ROWS, dtype=jnp.int32) - (ROWS - TH)
    bits = jnp.where(local < 0, 1, bits)
    bits = jnp.where(local == first, 1, bits)
    bits = jnp.where(local == second, 0, bits)
    return bits.astype(jnp.int32)


def levels(rng, dims, cuts, least, top_value):
    def one(dim, parts):
        heights = jax.random.uniform(jax.random.fold_in(jax.random.fold_in(rng, 6), dim), (parts,), jnp.float32, least / len(cuts), top_value / len(cuts))
        return jnp.repeat(jnp.exp(heights), dims[dim] // parts).reshape((-1,) + (1,) * (len(dims) - dim - 1))

    gain = one(*cuts[0])
    for cut in cuts[1:]:
        gain = gain * one(*cut)
    return gain


def normal_values(stream_key, shape, deviation, most, cuts=(), kind=jnp.bfloat16):
    values = deviation * jax.random.normal(stream_key, shape, jnp.float32)
    if cuts:
        values = values * levels(stream_key, shape, cuts, -0.22, 0.18)
    return jnp.clip(values, -most, most).astype(kind)


def setup_inputs(seed: int = 0) -> dict:
    arg_keys = jax.random.split(jax.random.key(seed), 7)
    query_heads = draw_query_heads(jax.random.fold_in(arg_keys[6], 71), 0)
    key_heads = draw_key_heads(jax.random.fold_in(arg_keys[6], 71), 0)
    value_heads = draw_value_heads(jax.random.fold_in(arg_keys[6], 71), 0)
    row_valid = draw_row_valid(jax.random.fold_in(arg_keys[6], 71), 0)
    out_weight = normal_values(arg_keys[4], (HEADS * HD, D), (HEADS * HD) ** -0.5, 0.375, ((1, 2),))
    grad_mixed = normal_values(arg_keys[5], (FRAMES, ROWS, COLS, D), 1.0, 6.0, ((0, 4), (2, 4), (3, 2)))
    return dict(query_heads=query_heads, key_heads=key_heads, value_heads=value_heads, row_valid=row_valid, out_weight=out_weight, grad_mixed=grad_mixed)


NEG_FILL = -1e+30

def band_layout(tile_count):
    band_tiles = min(4, tile_count)
    layout = []
    for band_index in range(tile_count // 2):
        key_tile = min(max(2 * band_index - 1, 0), tile_count - band_tiles)
        layout.append((2 * band_index, key_tile, band_tiles))
    return layout

def tile_number(frames, rows, columns, row_start, tile_rows):
    row_ids = lax.broadcasted_iota(jnp.int32, (frames, rows, columns), 1)
    return ((row_ids + row_start) // tile_rows).reshape(-1)

def band_parts(query_block, key_wide, value_wide, live_wide, tile_rows, scale, entry):
    query_tile, key_tile, band_tiles = entry
    frames, rows, columns, depth = query_block.shape
    query_low = query_tile * tile_rows
    key_low = key_tile * tile_rows
    key_rows = band_tiles * tile_rows
    query_band = query_block[:, query_low:query_low + 2 * tile_rows].reshape(-1, depth)
    key_band = key_wide[:, key_low:key_low + key_rows].reshape(-1, depth)
    value_band = value_wide[:, key_low:key_low + key_rows].reshape(-1, depth)
    live_band = live_wide[:, key_low:key_low + key_rows].reshape(-1)
    query_tiles = tile_number(frames, 2 * tile_rows, columns, query_low, tile_rows)
    key_tiles = tile_number(key_wide.shape[0], key_rows, key_wide.shape[2], key_low, tile_rows)
    allowed = live_band[None, :] & (jnp.abs(query_tiles[:, None] - key_tiles[None, :]) <= 1)
    scores = jnp.dot(query_band, key_band.T, preferred_element_type=jnp.float32) * scale
    scores = jnp.where(allowed, scores, NEG_FILL)
    return (query_band, key_band, value_band, scores)

def attend_forward(query_block, key_wide, value_wide, live_wide, tile_rows, scale):
    frames, rows, columns, depth = query_block.shape
    outputs = []
    logs = []
    for entry in band_layout(rows // tile_rows):
        query_band, key_band, value_band, scores = band_parts(query_block, key_wide, value_wide, live_wide, tile_rows, scale, entry)
        peak = lax.optimization_barrier(jnp.max(scores, axis=1, keepdims=True))
        expos = jnp.exp(scores - peak)
        totals = lax.optimization_barrier(jnp.sum(expos, axis=1, keepdims=True))
        attended = jnp.dot(expos.astype(jnp.bfloat16), value_band, preferred_element_type=jnp.float32) / totals
        outputs.append(attended.astype(jnp.bfloat16).reshape(frames, 2 * tile_rows, columns, depth))
        logs.append((peak + jnp.log(totals)).reshape(frames, 2 * tile_rows, columns))
    return (jnp.concatenate(outputs, axis=1), jnp.concatenate(logs, axis=1))

def attend_backward(query_block, key_wide, value_wide, live_wide, lse_block, grad_block, delta_block, tile_rows, scale):
    frames, rows, columns, depth = query_block.shape
    wide_frames = key_wide.shape[0]
    wide_columns = key_wide.shape[2]
    grad_pair = jnp.zeros((2, wide_frames, rows, wide_columns, depth), jnp.float32)
    grad_parts = []
    for entry in band_layout(rows // tile_rows):
        query_tile, key_tile, band_tiles = entry
        query_low = query_tile * tile_rows
        key_low = key_tile * tile_rows
        key_rows = band_tiles * tile_rows
        query_band, key_band, value_band, scores = band_parts(query_block, key_wide, value_wide, live_wide, tile_rows, scale, entry)
        lse_band = lse_block[:, query_low:query_low + 2 * tile_rows].reshape(-1)
        delta_band = delta_block[:, query_low:query_low + 2 * tile_rows].reshape(-1)
        grad_band = grad_block[:, query_low:query_low + 2 * tile_rows].reshape(-1, depth)
        probs = jnp.exp(scores - lse_band[:, None])
        dprob = jnp.dot(grad_band, value_band.T, preferred_element_type=jnp.float32)
        dscore = (probs * (dprob - delta_band[:, None]) * scale).astype(jnp.bfloat16)
        grad_query_band = jnp.dot(dscore, key_band, preferred_element_type=jnp.float32)
        grad_key_band = jnp.dot(dscore.T, query_band, preferred_element_type=jnp.float32)
        grad_value_band = jnp.dot(probs.astype(jnp.bfloat16).T, grad_band, preferred_element_type=jnp.float32)
        grad_pair = grad_pair.at[0, :, key_low:key_low + key_rows].add(grad_key_band.reshape(wide_frames, key_rows, wide_columns, depth))
        grad_pair = grad_pair.at[1, :, key_low:key_low + key_rows].add(grad_value_band.reshape(wide_frames, key_rows, wide_columns, depth))
        grad_parts.append(grad_query_band.reshape(frames, 2 * tile_rows, columns, depth))
    return (jnp.concatenate(grad_parts, axis=1), grad_pair)

def reference(query_heads, key_heads, value_heads, row_valid, out_weight, grad_mixed):
    scale = 1.0 / math.sqrt(HD)
    frames_all, rows_all, columns_all, head_width = query_heads.shape
    block_count = N_TM * N_WIDTH
    pad_sizes = ((TF, TF), (0, 0), (TW, TW), (0, 0))
    live_rows = row_valid > 0
    zero = jnp.zeros((), jnp.int32)
    frame_step = jnp.asarray(TF).astype(jnp.int32)
    column_step = jnp.asarray(TW).astype(jnp.int32)

    def live_for(block_time, block_column):
        frame_ids = (block_time - 1) * frame_step + jnp.arange(3 * TF, dtype=jnp.int32)
        column_ids = (block_column - 1) * column_step + jnp.arange(3 * TW, dtype=jnp.int32)
        frame_ok = (frame_ids >= 0) & (frame_ids < frames_all)
        column_ok = (column_ids >= 0) & (column_ids < columns_all)
        return frame_ok[:, None, None] & live_rows[None, :, None] & column_ok[None, None, :]
    head_outputs = []
    head_logs = []
    for head_index in range(HEADS):
        low = head_index * HD
        query_one = query_heads[..., low:low + HD]
        key_padded = jnp.pad(key_heads[..., low:low + HD], pad_sizes)
        value_padded = jnp.pad(value_heads[..., low:low + HD], pad_sizes)

        def forward_step(block_index, carry):
            out_all, lse_all = carry
            block_index = jnp.asarray(block_index).astype(jnp.int32)
            block_time = block_index // N_WIDTH
            block_column = block_index % N_WIDTH
            corner = (block_time * frame_step, zero, block_column * column_step, zero)
            query_block = lax.dynamic_slice(query_one, corner, (TF, rows_all, TW, HD))
            key_wide = lax.dynamic_slice(key_padded, corner, (3 * TF, rows_all, 3 * TW, HD))
            value_wide = lax.dynamic_slice(value_padded, corner, (3 * TF, rows_all, 3 * TW, HD))
            attended, lse_block = attend_forward(query_block, key_wide, value_wide, live_for(block_time, block_column), TH, scale)
            out_all = lax.dynamic_update_slice(out_all, attended, corner)
            lse_all = lax.dynamic_update_slice(lse_all, lse_block, corner[:3])
            return (out_all, lse_all)
        start = (jnp.zeros((frames_all, rows_all, columns_all, HD), jnp.bfloat16), jnp.zeros((frames_all, rows_all, columns_all), jnp.float32))
        out_all, lse_all = lax.fori_loop(0, block_count, forward_step, start)
        head_outputs.append(out_all)
        head_logs.append(lse_all)
    attended_all = jnp.concatenate(head_outputs, axis=-1)
    attended_flat = attended_all.reshape(-1, head_width)
    grad_flat = grad_mixed.reshape(-1, D)
    mixed = jnp.dot(attended_flat, out_weight, preferred_element_type=jnp.float32).astype(jnp.bfloat16).reshape(frames_all, rows_all, columns_all, D)
    grad_weight = jnp.dot(attended_flat.T, grad_flat, preferred_element_type=jnp.float32)
    grad_attended = jnp.dot(grad_flat, out_weight.T, preferred_element_type=jnp.float32).astype(jnp.bfloat16).reshape(frames_all, rows_all, columns_all, head_width)
    query_grads = []
    key_grads = []
    value_grads = []
    for head_index in range(HEADS):
        low = head_index * HD
        query_one = query_heads[..., low:low + HD]
        key_padded = jnp.pad(key_heads[..., low:low + HD], pad_sizes)
        value_padded = jnp.pad(value_heads[..., low:low + HD], pad_sizes)
        grad_one = grad_attended[..., low:low + HD]
        delta_one = lax.optimization_barrier(jnp.sum(grad_one.astype(jnp.float32) * head_outputs[head_index].astype(jnp.float32), axis=-1))
        lse_one = head_logs[head_index]

        def backward_step(block_index, carry):
            grad_query_all, grad_pair_all = carry
            block_index = jnp.asarray(block_index).astype(jnp.int32)
            block_time = block_index // N_WIDTH
            block_column = block_index % N_WIDTH
            corner = (block_time * frame_step, zero, block_column * column_step, zero)
            query_block = lax.dynamic_slice(query_one, corner, (TF, rows_all, TW, HD))
            key_wide = lax.dynamic_slice(key_padded, corner, (3 * TF, rows_all, 3 * TW, HD))
            value_wide = lax.dynamic_slice(value_padded, corner, (3 * TF, rows_all, 3 * TW, HD))
            grad_block = lax.dynamic_slice(grad_one, corner, (TF, rows_all, TW, HD))
            lse_block = lax.dynamic_slice(lse_one, corner[:3], (TF, rows_all, TW))
            delta_block = lax.dynamic_slice(delta_one, corner[:3], (TF, rows_all, TW))
            grad_query_block, grad_pair = attend_backward(query_block, key_wide, value_wide, live_for(block_time, block_column), lse_block, grad_block, delta_block, TH, scale)
            grad_query_all = lax.dynamic_update_slice(grad_query_all, grad_query_block.astype(jnp.bfloat16), corner)
            pair_corner = (zero, block_time * frame_step, zero, block_column * column_step, zero)
            current = lax.dynamic_slice(grad_pair_all, pair_corner, (2, 3 * TF, rows_all, 3 * TW, HD))
            grad_pair_all = lax.dynamic_update_slice(grad_pair_all, current + grad_pair, pair_corner)
            return (grad_query_all, grad_pair_all)
        start = (jnp.zeros((frames_all, rows_all, columns_all, HD), jnp.bfloat16), jnp.zeros((2, frames_all + 2 * TF, rows_all, columns_all + 2 * TW, HD), jnp.float32))
        grad_query_all, grad_pair_all = lax.fori_loop(0, block_count, backward_step, start)
        inner = grad_pair_all[:, TF:TF + frames_all, :, TW:TW + columns_all]
        query_grads.append(grad_query_all)
        key_grads.append(inner[0].astype(jnp.bfloat16))
        value_grads.append(inner[1].astype(jnp.bfloat16))
    grad_query = jnp.concatenate(query_grads, axis=-1)
    grad_key = jnp.concatenate(key_grads, axis=-1)
    grad_value = jnp.concatenate(value_grads, axis=-1)
    return (mixed, grad_query, grad_key, grad_value, grad_weight)
```

```python
import functools
import math

import jax
import jax.numpy as jnp
from jax import lax
from jax.experimental import pallas as pl
from jax.experimental.pallas import tpu as pltpu
from jax.sharding import PartitionSpec as P

TH = 9
FAR = 1e30
LOG2E = 1.4426950408889634


def round_up(value, step):
    return -(-value // step) * step


def dot_nt(left, right):
    return lax.dot_general(
        left, right, (((1,), (1,)), ((), ())), preferred_element_type=jnp.float32
    )


def gather_tiles(pieces, dests, sems, block):
    copies = []
    index = 0
    for piece in pieces:
        for which, dest in enumerate(dests):
            copies.append((piece.at[which], dest))
    started = []
    for index, (source, dest) in enumerate(copies):
        slot = index // len(dests)
        copy = pltpu.make_async_copy(
            source, dest.at[:, slot * block : (slot + 1) * block, :], sems.at[index]
        )
        copy.start()
        started.append(copy)
    return started


def split_pieces(own, near, far):
    views = [own]
    views += list(near)
    for pair in far:
        views += [pair.at[0], pair.at[1]]
    return views


def query_kernel(
    q_ref, g_ref, bias_ref, own, t_prev, t_next, w_prev, w_next, c_prev, c_next,
    att_ref, gq_ref, stats_ref,
    k_all, v_all, s_buf, top, tot, out, grad, sems,
    *, tiles, block, wide, chunk, scale,
):
    per = wide // chunk
    depth = q_ref.shape[-1]
    fill = jnp.zeros((tiles, wide - 9 * block, depth), jnp.bfloat16)
    k_all[:, 9 * block :, :] = fill
    v_all[:, 9 * block :, :] = fill
    pieces = split_pieces(own, (t_prev, t_next, w_prev, w_next), (c_prev, c_next))
    for copy in gather_tiles(pieces, (k_all, v_all), sems, block):
        copy.wait()

    @pl.loop(0, tiles)
    def _(tile):
        low = jnp.maximum(tile - 1, 0) * per
        high = (jnp.minimum(tile + 1, tiles - 1) + 1) * per
        top[...] = jnp.full(top.shape, -3e38, jnp.float32)
        tot[...] = jnp.zeros(tot.shape, jnp.float32)
        out[...] = jnp.zeros(out.shape, jnp.float32)
        grad[...] = jnp.zeros(grad.shape, jnp.float32)

        @pl.loop(low, high)
        def _(step):
            row = step // per
            start = pl.multiple_of((step % per) * chunk, chunk)
            keys = k_all[row, pl.ds(start, chunk), :]
            scores = dot_nt(q_ref[tile], keys) * (scale * LOG2E)
            scores = scores + bias_ref[row, :, pl.ds(start, chunk)]
            s_buf[step - low] = scores
            best = top[...]
            for lane in range(0, chunk, 128):
                best = jnp.maximum(best, scores[:, lane : lane + 128])
            top[...] = best

        peak = jnp.max(top[...], axis=1, keepdims=True)

        @pl.loop(low, high)
        def _(step):
            row = step // per
            start = pl.multiple_of((step % per) * chunk, chunk)
            expos = jnp.exp2(s_buf[step - low] - peak)
            s_buf[step - low] = expos
            part = tot[...]
            for lane in range(0, chunk, 128):
                part = part + expos[:, lane : lane + 128]
            tot[...] = part
            out[...] += jnp.dot(
                expos.astype(jnp.bfloat16),
                v_all[row, pl.ds(start, chunk), :],
                preferred_element_type=jnp.float32,
            )

        total = jnp.sum(tot[...], axis=1, keepdims=True)
        attended = (out[...] / total).astype(jnp.bfloat16)
        att_ref[tile] = attended
        delta = jnp.sum(
            g_ref[tile].astype(jnp.float32) * attended.astype(jnp.float32), axis=1, keepdims=True
        )
        lanes = lax.broadcasted_iota(jnp.int32, (block, 128), 1)
        stats_ref[tile] = jnp.where(lanes == 0, peak + jnp.log2(total), delta)

        @pl.loop(low, high)
        def _(step):
            row = step // per
            start = pl.multiple_of((step % per) * chunk, chunk)
            dprob = dot_nt(g_ref[tile], v_all[row, pl.ds(start, chunk), :])
            dscore = (s_buf[step - low] * (dprob - delta)).astype(jnp.bfloat16)
            grad[...] += jnp.dot(
                dscore, k_all[row, pl.ds(start, chunk), :], preferred_element_type=jnp.float32
            )

        gq_ref[tile] = (grad[...] * (scale / total)).astype(jnp.bfloat16)


def key_kernel(
    k_ref, v_ref, live_ref, stats_ref, own, t_prev, t_next, w_prev, w_next, c_prev, c_next,
    gk_ref, gv_ref,
    q_all, g_all, grad_k, grad_v, sems,
    *, tiles, block, wide, chunk, scale,
):
    per = wide // chunk
    depth = k_ref.shape[-1]
    fill = jnp.zeros((tiles, wide - 9 * block, depth), jnp.bfloat16)
    q_all[:, 9 * block :, :] = fill
    g_all[:, 9 * block :, :] = fill
    pieces = split_pieces(own, (t_prev, t_next, w_prev, w_next), (c_prev, c_next))
    for copy in gather_tiles(pieces, (q_all, g_all), sems, block):
        copy.wait()

    @pl.loop(0, tiles)
    def _(tile):
        low = jnp.maximum(tile - 1, 0) * per
        high = (jnp.minimum(tile + 1, tiles - 1) + 1) * per
        grad_k[...] = jnp.zeros(grad_k.shape, jnp.float32)
        grad_v[...] = jnp.zeros(grad_v.shape, jnp.float32)

        @pl.loop(low, high)
        def _(step):
            row = step // per
            start = pl.multiple_of((step % per) * chunk, chunk)
            queries = q_all[row, pl.ds(start, chunk), :]
            grads = g_all[row, pl.ds(start, chunk), :]
            lse = stats_ref[row, 0:1, pl.ds(start, chunk)]
            delta = stats_ref[row, 1:2, pl.ds(start, chunk)]
            probs = jnp.exp2(dot_nt(k_ref[tile], queries) * (scale * LOG2E) - lse)
            grad_v[...] += jnp.dot(
                probs.astype(jnp.bfloat16), grads, preferred_element_type=jnp.float32
            )
            dscore = probs * (dot_nt(v_ref[tile], grads) - delta)
            grad_k[...] += jnp.dot(
                dscore.astype(jnp.bfloat16), queries, preferred_element_type=jnp.float32
            )

        live = live_ref[tile] > 0
        gk_ref[tile] = jnp.where(live, grad_k[...] * scale, 0.0).astype(jnp.bfloat16)
        gv_ref[tile] = jnp.where(live, grad_v[...], 0.0).astype(jnp.bfloat16)


def shift(cells, axis, forward):
    count = lax.axis_size(axis)
    if forward:
        pairs = [(i, i + 1) for i in range(count - 1)]
    else:
        pairs = [(i + 1, i) for i in range(count - 1)]
    return lax.ppermute(cells, axis, pairs)


def neighbours(cells):
    t_prev = shift(cells, "tm", True)
    t_next = shift(cells, "tm", False)
    w_prev = shift(cells, "width", True)
    w_next = shift(cells, "width", False)
    pair = jnp.stack([t_prev, t_next])
    return (
        cells, t_prev, t_next, w_prev, w_next,
        shift(pair, "width", True), shift(pair, "width", False),
    )


def lay_out(cells, block, tile_rows):
    frames, columns, rows, depth = cells.shape
    tiles = rows // tile_rows
    cells = cells.reshape(frames * columns, tiles, tile_rows, depth).transpose(1, 0, 2, 3)
    cells = cells.reshape(tiles, frames * columns * tile_rows, depth)
    return jnp.pad(cells, ((0, 0), (0, block - cells.shape[1]), (0, 0)))


def lay_back(cells, frames, columns, tile_rows):
    tiles, _, depth = cells.shape
    count = frames * columns
    cells = cells[:, : count * tile_rows].reshape(tiles, count, tile_rows, depth)
    return cells.transpose(1, 0, 2, 3).reshape(frames, columns, tiles * tile_rows, depth)


def shards(query_heads, key_heads, value_heads, row_valid, out_weight, grad_mixed):
    frames, rows, columns, depth = query_heads.shape
    scale = 1.0 / math.sqrt(depth)
    tiles = rows // TH
    count = frames * columns * TH
    block = round_up(count, 16)
    wide = round_up(9 * block, 256)
    chunk = wide // 2
    swap = (0, 2, 1, 3)
    query = lay_out(query_heads.transpose(swap), block, TH)
    key = lay_out(key_heads.transpose(swap), block, TH)
    value = lay_out(value_heads.transpose(swap), block, TH)
    grad_in = grad_mixed.transpose(swap)

    t_index, w_index = lax.axis_index("tm"), lax.axis_index("width")
    t_back, t_ahead = t_index > 0, t_index < lax.axis_size("tm") - 1
    w_back, w_ahead = w_index > 0, w_index < lax.axis_size("width") - 1
    exists = jnp.stack([
        t_index >= 0, t_back, t_ahead, w_back, w_ahead,
        t_back & w_back, t_ahead & w_back, t_back & w_ahead, t_ahead & w_ahead,
    ])
    live = jnp.broadcast_to(
        (row_valid > 0).reshape(tiles, 1, TH), (tiles, frames * columns, TH)
    ).reshape(tiles, count)
    live = jnp.pad(live, ((0, 0), (0, block - count)))
    wide_live = (live[:, None, :] & exists[None, :, None]).reshape(tiles, 9 * block)
    wide_live = jnp.pad(wide_live, ((0, 0), (0, wide - 9 * block)))
    bias = jnp.where(wide_live, 0.0, -FAR).astype(jnp.float32)[:, None, :]

    key_value = neighbours(jnp.stack([key, value]))
    grad_heads = lax.dot_general(
        grad_in, out_weight, (((3,), (1,)), ((), ())), preferred_element_type=jnp.float32
    )
    grad_own = lax.psum_scatter(
        grad_heads.astype(jnp.bfloat16), "head", scatter_dimension=3, tiled=True
    )
    grad_own = lay_out(grad_own, block, TH)
    query_grad = neighbours(jnp.stack([query, grad_own]))

    pairs = tiles * 3 - 2
    work = pairs * block * wide
    in_vmem = pl.BlockSpec(memory_space=pltpu.VMEM)
    in_any = pl.BlockSpec(memory_space=pl.ANY)
    params = dict(tiles=tiles, block=block, wide=wide, chunk=chunk, scale=scale)
    flat = jax.ShapeDtypeStruct((tiles, block, depth), jnp.bfloat16)
    wide_bf16 = pltpu.VMEM((tiles, wide, depth), jnp.bfloat16)
    acc = pltpu.VMEM((block, depth), jnp.float32)
    lane_acc = pltpu.VMEM((block, 128), jnp.float32)
    cost = pl.CostEstimate(
        flops=16 * work * depth, transcendentals=work, bytes_accessed=4 * tiles * wide * depth
    )
    attended, grad_query, stats = pl.pallas_call(
        functools.partial(query_kernel, **params),
        out_shape=(flat, flat, jax.ShapeDtypeStruct((tiles, block, 128), jnp.float32)),
        in_specs=[in_vmem] * 3 + [in_any] * 7,
        out_specs=(in_vmem, in_vmem, in_vmem),
        scratch_shapes=[
            wide_bf16, wide_bf16,
            pltpu.VMEM((min(3, tiles) * (wide // chunk), block, chunk), jnp.float32),
            lane_acc, lane_acc, acc, acc,
            pltpu.SemaphoreType.DMA((18,)),
        ],
        compiler_params=pltpu.CompilerParams(vmem_limit_bytes=50 << 20),
        cost_estimate=cost,
        name="query_side",
    )(query, grad_own, bias, *key_value)

    stats_own = stats[:, :, :2].transpose(0, 2, 1)
    near = neighbours(stats_own)
    joined = jnp.stack(list(near[:5]) + [near[5][0], near[5][1], near[6][0], near[6][1]], axis=2)
    blank = jnp.array([FAR, 0.0], jnp.float32)[None, :, None, None]
    joined = jnp.where(exists[None, None, :, None], joined, blank).reshape(tiles, 2, 9 * block)
    tail = jnp.broadcast_to(blank[..., 0], (tiles, 2, wide - 9 * block))
    stats_wide = jnp.concatenate([joined, tail], axis=2)

    attended = lay_back(attended, frames, columns, TH)
    other = lax.ppermute(attended, "head", [(0, 1), (1, 0)])
    first = lax.axis_index("head") == 0
    heads_all = jnp.concatenate(
        [jnp.where(first, attended, other), jnp.where(first, other, attended)], axis=3
    )
    mixed = lax.dot_general(
        heads_all, out_weight, (((3,), (0,)), ((), ())), preferred_element_type=jnp.float32
    ).astype(jnp.bfloat16)
    grad_weight = lax.psum_scatter(
        lax.dot_general(
            heads_all, grad_in, (((0, 1, 2), (0, 1, 2)), ((), ())),
            preferred_element_type=jnp.float32,
        ),
        ("tm", "width"), scatter_dimension=0, tiled=True,
    )

    live_rows = live.astype(jnp.float32)[:, :, None]
    grad_key, grad_value = pl.pallas_call(
        functools.partial(key_kernel, **params),
        out_shape=(flat, flat),
        in_specs=[in_vmem] * 4 + [in_any] * 7,
        out_specs=(in_vmem, in_vmem),
        scratch_shapes=[wide_bf16, wide_bf16, acc, acc, pltpu.SemaphoreType.DMA((18,))],
        compiler_params=pltpu.CompilerParams(vmem_limit_bytes=50 << 20),
        cost_estimate=cost,
        name="key_side",
    )(key, value, live_rows, stats_wide, *query_grad)

    back = lambda cells: lay_back(cells, frames, columns, TH).transpose(swap)
    return (mixed.transpose(swap), back(grad_query), back(grad_key), back(grad_value), grad_weight)


def solution(mesh):
    split = P("tm", None, "width", "head")
    return jax.shard_map(
        shards,
        mesh=mesh,
        in_specs=(split, split, split, P(), P(None, "head"), split),
        out_specs=(split, split, split, split, P(("tm", "width"), "head")),
        check_vma=False,
    )
```

```python
import functools
import math

import jax
import jax.numpy as jnp
from jax import lax
from jax.experimental import pallas as pl
from jax.experimental.pallas import tpu as pltpu
from jax.sharding import PartitionSpec as P

TH = 9
FAR = 1e30
LOG2E = 1.4426950408889634


def round_up(value, step):
    return -(-value // step) * step


def dot_nt(left, right):
    return lax.dot_general(
        left, right, (((1,), (1,)), ((), ())), preferred_element_type=jnp.float32
    )


MESH = pl.DeviceIdType.MESH


def query_kernel(
    k_ref, v_ref, q_ref, part_own, part_other, bias_ref,
    att_ref, other_ref, gq_ref, q_all, g_all, stats_ref,
    k_all, v_all, s_buf, top, tot, out, grad, part_in, att_in, st_own, st_all,
    send_sem, recv_sem, own_sem, peer_send, peer_recv,
    *, tiles, block, wide, chunk, scale,
):
    per = wide // chunk
    depth = q_ref.shape[-1]
    t_index, w_index, h_index = (lax.axis_index(name) for name in ("tm", "width", "head"))
    t_back, t_ahead = t_index > 0, t_index < lax.axis_size("tm") - 1
    w_back, w_ahead = w_index > 0, w_index < lax.axis_size("width") - 1
    exists = [
        None, t_back, t_ahead, w_back, w_ahead,
        t_back & w_back, t_ahead & w_back, t_back & w_ahead, t_ahead & w_ahead,
    ]
    t_above = (t_index + 1, w_index, h_index)
    t_below = (t_index - 1, w_index, h_index)
    w_above = (t_index, w_index + 1, h_index)
    w_below = (t_index, w_index - 1, h_index)
    peer = (t_index, w_index, 1 - h_index)
    direct = [(1, t_ahead, t_above), (2, t_back, t_below), (3, w_ahead, w_above), (4, w_back, w_below)]
    onward = [
        (5, 1, t_back & w_ahead, w_above), (7, 1, t_back & w_back, w_below),
        (6, 2, t_ahead & w_ahead, w_above), (8, 2, t_ahead & w_back, w_below),
    ]

    def slot_of(which, slot):
        if which == 4:
            return st_all.at[slot]
        dest = (k_all, v_all, q_all, g_all)[which]
        return dest.at[:, slot * block : (slot + 1) * block, :]

    def remote(which, source, slot, device):
        return pltpu.make_async_remote_copy(
            src_ref=source, dst_ref=slot_of(which, slot),
            send_sem=send_sem.at[which, slot], recv_sem=recv_sem.at[which, slot],
            device_id=device, device_id_type=MESH,
        )

    def send_direct(which, source):
        for slot, there, device in direct:
            @pl.when(there)
            def _():
                remote(which, source, slot, device).start()

    def send_onward(which):
        for slot, via, there, device in onward:
            @pl.when(there)
            def _():
                remote(which, slot_of(which, via), slot, device).start()

    def receive(which, slots):
        for slot in slots:
            @pl.when(exists[slot])
            def _():
                remote(which, slot_of(which, slot), slot, peer).wait_recv()

    def sent(which, source):
        for slot, there, device in direct:
            @pl.when(there)
            def _():
                remote(which, source, slot, device).wait_send()
        for slot, via, there, device in onward:
            @pl.when(there)
            def _():
                remote(which, slot_of(which, via), slot, device).wait_send()

    barrier = pltpu.get_barrier_semaphore()
    for _, there, device in direct:
        @pl.when(there)
        def _():
            pl.semaphore_signal(barrier, inc=1, device_id=device, device_id_type=MESH)
    pl.semaphore_signal(barrier, inc=1, device_id=peer, device_id_type=MESH)
    greeted = 1 + sum(jnp.where(there, 1, 0) for _, there, _ in direct)
    pl.semaphore_wait(barrier, greeted)

    def swap_part():
        return pltpu.make_async_remote_copy(
            src_ref=part_other, dst_ref=part_in, send_sem=peer_send.at[0],
            recv_sem=peer_recv.at[0], device_id=peer, device_id_type=MESH,
        )

    def swap_att():
        return pltpu.make_async_remote_copy(
            src_ref=att_ref, dst_ref=att_in, send_sem=peer_send.at[1],
            recv_sem=peer_recv.at[1], device_id=peer, device_id_type=MESH,
        )

    swap_part().start()
    send_direct(0, k_ref)
    send_direct(1, v_ref)
    for which, source in enumerate((k_ref, v_ref, q_ref)):
        pltpu.make_async_copy(source, slot_of(which, 0), own_sem.at[which]).start()
    fill = jnp.zeros((tiles, wide - 9 * block, depth), jnp.bfloat16)
    hole = jnp.zeros((tiles, block, depth), jnp.bfloat16)
    for dest in (k_all, v_all, q_all, g_all):
        dest[:, 9 * block :, :] = fill
        for slot in range(1, 9):
            @pl.when(jnp.logical_not(exists[slot]))
            def _():
                dest[:, slot * block : (slot + 1) * block, :] = hole
    swap_part().wait()
    g_all[:, :block, :] = (
        part_own[...].astype(jnp.float32) + part_in[...].astype(jnp.float32)
    ).astype(jnp.bfloat16)
    for which, source in enumerate((k_ref, v_ref, q_ref)):
        pltpu.make_async_copy(source, slot_of(which, 0), own_sem.at[which]).wait()
    receive(0, (1, 2))
    send_onward(0)
    receive(1, (1, 2))
    send_onward(1)
    send_direct(2, q_ref)
    send_direct(3, slot_of(3, 0))
    receive(0, (3, 4, 5, 6, 7, 8))
    receive(1, (3, 4, 5, 6, 7, 8))

    @pl.loop(0, tiles)
    def _(tile):
        low = jnp.maximum(tile - 1, 0) * per
        high = (jnp.minimum(tile + 1, tiles - 1) + 1) * per
        top[...] = jnp.full(top.shape, -3e38, jnp.float32)
        tot[...] = jnp.zeros(tot.shape, jnp.float32)
        out[...] = jnp.zeros(out.shape, jnp.float32)
        grad[...] = jnp.zeros(grad.shape, jnp.float32)

        @pl.when(tile == tiles // 2)
        def _():
            for which in (2, 3):
                receive(which, (1, 2))
                send_onward(which)

        @pl.loop(low, high)
        def _(step):
            row = step // per
            start = pl.multiple_of((step % per) * chunk, chunk)
            keys = k_all[row, pl.ds(start, chunk), :]
            scores = dot_nt(q_ref[tile], keys) * (scale * LOG2E)
            scores = scores + bias_ref[row, :, pl.ds(start, chunk)]
            s_buf[step - low] = scores
            best = top[...]
            for lane in range(0, chunk, 128):
                best = jnp.maximum(best, scores[:, lane : lane + 128])
            top[...] = best

        peak = jnp.max(top[...], axis=1, keepdims=True)

        @pl.loop(low, high)
        def _(step):
            row = step // per
            start = pl.multiple_of((step % per) * chunk, chunk)
            expos = jnp.exp2(s_buf[step - low] - peak)
            s_buf[step - low] = expos
            part = tot[...]
            for lane in range(0, chunk, 128):
                part = part + expos[:, lane : lane + 128]
            tot[...] = part
            out[...] += jnp.dot(
                expos.astype(jnp.bfloat16),
                v_all[row, pl.ds(start, chunk), :],
                preferred_element_type=jnp.float32,
            )

        grads = g_all[tile, :block, :]
        total = jnp.sum(tot[...], axis=1, keepdims=True)
        attended = (out[...] / total).astype(jnp.bfloat16)
        att_ref[tile] = attended
        delta = jnp.sum(
            grads.astype(jnp.float32) * attended.astype(jnp.float32), axis=1, keepdims=True
        )
        lanes = lax.broadcasted_iota(jnp.int32, (block, 128), 1)
        columns = jnp.where(lanes == 0, peak + jnp.log2(total), delta)
        span = st_own.shape[-1]
        columns = jnp.concatenate([columns, jnp.zeros((span - block, 128), jnp.float32)], axis=0)
        st_own[tile] = columns.T[:8]

        @pl.loop(low, high)
        def _(step):
            row = step // per
            start = pl.multiple_of((step % per) * chunk, chunk)
            dprob = dot_nt(grads, v_all[row, pl.ds(start, chunk), :])
            dscore = (s_buf[step - low] * (dprob - delta)).astype(jnp.bfloat16)
            grad[...] += jnp.dot(
                dscore, k_all[row, pl.ds(start, chunk), :], preferred_element_type=jnp.float32
            )

        gq_ref[tile] = (grad[...] * (scale / total)).astype(jnp.bfloat16)

    swap_att().start()
    send_direct(4, st_own)
    first = lax.broadcasted_iota(jnp.int32, (tiles, 8, wide), 1) == 0
    stats_ref[...] = jnp.where(first, FAR, 0.0)
    stats_ref[:, :, :block] = st_own[:, :, :block]
    receive(4, (1, 2))
    send_onward(4)
    for which in (2, 3, 4):
        receive(which, (3, 4, 5, 6, 7, 8))
    for slot in range(1, 9):
        @pl.when(exists[slot])
        def _():
            stats_ref[:, :, slot * block : (slot + 1) * block] = st_all[slot, :, :, :block]
    for which, source in enumerate((k_ref, v_ref, q_ref, slot_of(3, 0), st_own)):
        sent(which, source)
    swap_att().wait()
    other_ref[...] = att_in[...]


def key_kernel(
    k_ref, v_ref, live_ref, stats_ref, q_all, g_all, gk_ref, gv_ref, grad_k, grad_v,
    *, tiles, block, wide, chunk, scale,
):
    per = wide // chunk

    @pl.loop(0, tiles)
    def _(tile):
        low = jnp.maximum(tile - 1, 0) * per
        high = (jnp.minimum(tile + 1, tiles - 1) + 1) * per
        grad_k[...] = jnp.zeros(grad_k.shape, jnp.float32)
        grad_v[...] = jnp.zeros(grad_v.shape, jnp.float32)

        @pl.loop(low, high)
        def _(step):
            row = step // per
            start = pl.multiple_of((step % per) * chunk, chunk)
            queries = q_all[row, pl.ds(start, chunk), :]
            grads = g_all[row, pl.ds(start, chunk), :]
            lse = stats_ref[row, 0:1, pl.ds(start, chunk)]
            delta = stats_ref[row, 1:2, pl.ds(start, chunk)]
            probs = jnp.exp2(dot_nt(k_ref[tile], queries) * (scale * LOG2E) - lse)
            grad_v[...] += jnp.dot(
                probs.astype(jnp.bfloat16), grads, preferred_element_type=jnp.float32
            )
            dscore = probs * (dot_nt(v_ref[tile], grads) - delta)
            grad_k[...] += jnp.dot(
                dscore.astype(jnp.bfloat16), queries, preferred_element_type=jnp.float32
            )

        live = live_ref[tile] > 0
        gk_ref[tile] = jnp.where(live, grad_k[...] * scale, 0.0).astype(jnp.bfloat16)
        gv_ref[tile] = jnp.where(live, grad_v[...], 0.0).astype(jnp.bfloat16)


def lay_out(cells, block, tile_rows):
    frames, columns, rows, depth = cells.shape
    tiles = rows // tile_rows
    cells = cells.reshape(frames * columns, tiles, tile_rows, depth).transpose(1, 0, 2, 3)
    cells = cells.reshape(tiles, frames * columns * tile_rows, depth)
    return jnp.pad(cells, ((0, 0), (0, block - cells.shape[1]), (0, 0)))


def lay_back(cells, frames, columns, tile_rows):
    tiles, _, depth = cells.shape
    count = frames * columns
    cells = cells[:, : count * tile_rows].reshape(tiles, count, tile_rows, depth)
    return cells.transpose(1, 0, 2, 3).reshape(frames, columns, tiles * tile_rows, depth)


def shards(query_heads, key_heads, value_heads, row_valid, out_weight, grad_mixed):
    frames, rows, columns, depth = query_heads.shape
    scale = 1.0 / math.sqrt(depth)
    tiles = rows // TH
    count = frames * columns * TH
    block = round_up(count, 16)
    wide = round_up(9 * block, 256)
    chunk = wide // 2
    swap = (0, 2, 1, 3)
    query = lay_out(query_heads.transpose(swap), block, TH)
    key = lay_out(key_heads.transpose(swap), block, TH)
    value = lay_out(value_heads.transpose(swap), block, TH)
    grad_in = grad_mixed.transpose(swap)

    t_index, w_index = lax.axis_index("tm"), lax.axis_index("width")
    t_back, t_ahead = t_index > 0, t_index < lax.axis_size("tm") - 1
    w_back, w_ahead = w_index > 0, w_index < lax.axis_size("width") - 1
    exists = jnp.stack([
        t_index >= 0, t_back, t_ahead, w_back, w_ahead,
        t_back & w_back, t_ahead & w_back, t_back & w_ahead, t_ahead & w_ahead,
    ])
    live = jnp.broadcast_to(
        (row_valid > 0).reshape(tiles, 1, TH), (tiles, frames * columns, TH)
    ).reshape(tiles, count)
    live = jnp.pad(live, ((0, 0), (0, block - count)))
    wide_live = (live[:, None, :] & exists[None, :, None]).reshape(tiles, 9 * block)
    wide_live = jnp.pad(wide_live, ((0, 0), (0, wide - 9 * block)))
    bias = jnp.where(wide_live, 0.0, -FAR).astype(jnp.float32)[:, None, :]

    grad_heads = lax.dot_general(
        grad_in, out_weight, (((3,), (1,)), ((), ())), preferred_element_type=jnp.float32
    )
    parts = lay_out(grad_heads.astype(jnp.bfloat16), block, TH)
    low_part, high_part = parts[..., :depth], parts[..., depth:]
    first = lax.axis_index("head") == 0
    part_own = jnp.where(first, low_part, high_part)
    part_other = jnp.where(first, high_part, low_part)

    pairs = tiles * 3 - 2
    work = pairs * block * wide
    in_vmem = pl.BlockSpec(memory_space=pltpu.VMEM)
    params = dict(tiles=tiles, block=block, wide=wide, chunk=chunk, scale=scale)
    flat = jax.ShapeDtypeStruct((tiles, block, depth), jnp.bfloat16)
    wide_bf16 = pltpu.VMEM((tiles, wide, depth), jnp.bfloat16)
    acc = pltpu.VMEM((block, depth), jnp.float32)
    lane_acc = pltpu.VMEM((block, 128), jnp.float32)
    cost = pl.CostEstimate(
        flops=16 * work * depth, transcendentals=work, bytes_accessed=4 * tiles * wide * depth
    )
    spread = jax.ShapeDtypeStruct((tiles, wide, depth), jnp.bfloat16)
    span = round_up(block, 128)
    tile_bf16 = pltpu.VMEM((tiles, block, depth), jnp.bfloat16)
    attended, other, grad_query, query_wide, grad_wide, stats_wide = pl.pallas_call(
        functools.partial(query_kernel, **params),
        out_shape=(
            flat, flat, flat, spread, spread,
            jax.ShapeDtypeStruct((tiles, 8, wide), jnp.float32),
        ),
        in_specs=[in_vmem] * 6,
        out_specs=(in_vmem,) * 6,
        scratch_shapes=[
            wide_bf16, wide_bf16,
            pltpu.VMEM((min(3, tiles) * (wide // chunk), block, chunk), jnp.float32),
            lane_acc, lane_acc, acc, acc, tile_bf16, tile_bf16,
            pltpu.VMEM((tiles, 8, span), jnp.float32),
            pltpu.VMEM((9, tiles, 8, span), jnp.float32),
            pltpu.SemaphoreType.DMA((5, 9)),
            pltpu.SemaphoreType.DMA((5, 9)),
            pltpu.SemaphoreType.DMA((3,)),
            pltpu.SemaphoreType.DMA((2,)),
            pltpu.SemaphoreType.DMA((2,)),
        ],
        compiler_params=pltpu.CompilerParams(
            vmem_limit_bytes=56 << 20, collective_id=0, has_side_effects=True
        ),
        cost_estimate=cost,
        name="query_side",
    )(key, value, query, part_own, part_other, bias)

    attended = lay_back(attended, frames, columns, TH)
    other = lay_back(other, frames, columns, TH)
    heads_all = jnp.concatenate(
        [jnp.where(first, attended, other), jnp.where(first, other, attended)], axis=3
    )
    mixed = lax.dot_general(
        heads_all, out_weight, (((3,), (0,)), ((), ())), preferred_element_type=jnp.float32
    ).astype(jnp.bfloat16)
    grad_weight = lax.psum_scatter(
        lax.dot_general(
            heads_all, grad_in, (((0, 1, 2), (0, 1, 2)), ((), ())),
            preferred_element_type=jnp.float32,
        ),
        ("tm", "width"), scatter_dimension=0, tiled=True,
    )

    live_rows = live.astype(jnp.float32)[:, :, None]
    grad_key, grad_value = pl.pallas_call(
        functools.partial(key_kernel, **params),
        out_shape=(flat, flat),
        in_specs=[in_vmem] * 6,
        out_specs=(in_vmem, in_vmem),
        scratch_shapes=[acc, acc],
        compiler_params=pltpu.CompilerParams(vmem_limit_bytes=50 << 20),
        cost_estimate=cost,
        name="key_side",
    )(key, value, live_rows, stats_wide, query_wide, grad_wide)

    back = lambda cells: lay_back(cells, frames, columns, TH).transpose(swap)
    return (mixed.transpose(swap), back(grad_query), back(grad_key), back(grad_value), grad_weight)


def solution(mesh):
    split = P("tm", None, "width", "head")
    return jax.shard_map(
        shards,
        mesh=mesh,
        in_specs=(split, split, split, P(), P(None, "head"), split),
        out_specs=(split, split, split, split, P(("tm", "width"), "head")),
        check_vma=False,
    )
```

```python
import functools
import math

import jax
import jax.numpy as jnp
from jax import lax
from jax.experimental import pallas as pl
from jax.experimental.pallas import tpu as pltpu
from jax.sharding import PartitionSpec as P

TH = 9
FAR = 1e30
LOG2E = 1.4426950408889634


def round_up(value, step):
    return -(-value // step) * step


def dot_nt(left, right):
    return lax.dot_general(
        left, right, (((1,), (1,)), ((), ())), preferred_element_type=jnp.float32
    )


MESH = pl.DeviceIdType.MESH


def query_kernel(
    k_ref, v_ref, q_ref, part_own, part_other, bias_ref,
    att_ref, other_ref, gq_ref, q_all, g_all, stats_ref,
    k_all, v_all, s_buf, top, tot, out, grad, part_in, att_in, st_own, st_all,
    send_sem, recv_sem, own_sem, peer_send, peer_recv,
    *, tiles, block, wide, chunk, scale,
):
    per = wide // chunk
    depth = q_ref.shape[-1]
    t_index, w_index, h_index = (lax.axis_index(name) for name in ("tm", "width", "head"))
    t_back, t_ahead = t_index > 0, t_index < lax.axis_size("tm") - 1
    w_back, w_ahead = w_index > 0, w_index < lax.axis_size("width") - 1
    exists = [
        None, t_back, t_ahead, w_back, w_ahead,
        t_back & w_back, t_ahead & w_back, t_back & w_ahead, t_ahead & w_ahead,
    ]
    t_above = (t_index + 1, w_index, h_index)
    t_below = (t_index - 1, w_index, h_index)
    w_above = (t_index, w_index + 1, h_index)
    w_below = (t_index, w_index - 1, h_index)
    peer = (t_index, w_index, 1 - h_index)
    direct = [(1, t_ahead, t_above), (2, t_back, t_below), (3, w_ahead, w_above), (4, w_back, w_below)]
    onward = [
        (5, 1, t_back & w_ahead, w_above), (7, 1, t_back & w_back, w_below),
        (6, 2, t_ahead & w_ahead, w_above), (8, 2, t_ahead & w_back, w_below),
    ]

    def slot_of(which, slot):
        if which == 4:
            return st_all.at[slot]
        dest = (k_all, v_all, q_all, g_all)[which]
        return dest.at[:, slot * block : (slot + 1) * block, :]

    def remote(which, source, slot, device):
        return pltpu.make_async_remote_copy(
            src_ref=source, dst_ref=slot_of(which, slot),
            send_sem=send_sem.at[which, slot], recv_sem=recv_sem.at[which, slot],
            device_id=device, device_id_type=MESH,
        )

    def send_direct(which, source):
        for slot, there, device in direct:
            @pl.when(there)
            def _():
                remote(which, source, slot, device).start()

    def send_onward(which):
        for slot, via, there, device in onward:
            @pl.when(there)
            def _():
                remote(which, slot_of(which, via), slot, device).start()

    def receive(which, slots):
        for slot in slots:
            @pl.when(exists[slot])
            def _():
                remote(which, slot_of(which, slot), slot, peer).wait_recv()

    def sent(which, source):
        for slot, there, device in direct:
            @pl.when(there)
            def _():
                remote(which, source, slot, device).wait_send()
        for slot, via, there, device in onward:
            @pl.when(there)
            def _():
                remote(which, slot_of(which, via), slot, device).wait_send()

    barrier = pltpu.get_barrier_semaphore()
    for _, there, device in direct:
        @pl.when(there)
        def _():
            pl.semaphore_signal(barrier, inc=1, device_id=device, device_id_type=MESH)
    pl.semaphore_signal(barrier, inc=1, device_id=peer, device_id_type=MESH)
    greeted = 1 + sum(jnp.where(there, 1, 0) for _, there, _ in direct)
    pl.semaphore_wait(barrier, greeted)

    def swap_part():
        return pltpu.make_async_remote_copy(
            src_ref=part_other, dst_ref=part_in, send_sem=peer_send.at[0],
            recv_sem=peer_recv.at[0], device_id=peer, device_id_type=MESH,
        )

    def swap_att():
        return pltpu.make_async_remote_copy(
            src_ref=att_ref, dst_ref=att_in, send_sem=peer_send.at[1],
            recv_sem=peer_recv.at[1], device_id=peer, device_id_type=MESH,
        )

    swap_part().start()
    send_direct(0, k_ref)
    send_direct(1, v_ref)
    for which, source in enumerate((k_ref, v_ref, q_ref)):
        pltpu.make_async_copy(source, slot_of(which, 0), own_sem.at[which]).start()
    fill = jnp.zeros((tiles, wide - 9 * block, depth), jnp.bfloat16)
    hole = jnp.zeros((tiles, block, depth), jnp.bfloat16)
    for dest in (k_all, v_all, q_all, g_all):
        dest[:, 9 * block :, :] = fill
        for slot in range(1, 9):
            @pl.when(jnp.logical_not(exists[slot]))
            def _():
                dest[:, slot * block : (slot + 1) * block, :] = hole
    swap_part().wait()
    g_all[:, :block, :] = (
        part_own[...].astype(jnp.float32) + part_in[...].astype(jnp.float32)
    ).astype(jnp.bfloat16)
    for which, source in enumerate((k_ref, v_ref, q_ref)):
        pltpu.make_async_copy(source, slot_of(which, 0), own_sem.at[which]).wait()
    receive(0, (1, 2))
    send_onward(0)
    receive(1, (1, 2))
    send_onward(1)
    send_direct(2, q_ref)
    send_direct(3, slot_of(3, 0))
    receive(0, (3, 4, 5, 6, 7, 8))
    receive(1, (3, 4, 5, 6, 7, 8))

    @pl.loop(0, tiles)
    def _(tile):
        low = jnp.maximum(tile - 1, 0) * per
        high = (jnp.minimum(tile + 1, tiles - 1) + 1) * per
        top[...] = jnp.full(top.shape, -3e38, jnp.float32)
        tot[...] = jnp.zeros(tot.shape, jnp.float32)
        out[...] = jnp.zeros(out.shape, jnp.float32)
        grad[...] = jnp.zeros(grad.shape, jnp.float32)

        @pl.when(tile == tiles // 2)
        def _():
            for which in (2, 3):
                receive(which, (1, 2))
                send_onward(which)

        @pl.loop(low, high)
        def _(step):
            row = step // per
            start = pl.multiple_of((step % per) * chunk, chunk)
            keys = k_all[row, pl.ds(start, chunk), :]
            scores = dot_nt(q_ref[tile], keys) * (scale * LOG2E)
            scores = scores + bias_ref[row, :, pl.ds(start, chunk)]
            s_buf[step - low] = scores
            best = top[...]
            for lane in range(0, chunk, 128):
                best = jnp.maximum(best, scores[:, lane : lane + 128])
            top[...] = best

        peak = jnp.max(top[...], axis=1, keepdims=True)

        @pl.loop(low, high)
        def _(step):
            row = step // per
            start = pl.multiple_of((step % per) * chunk, chunk)
            expos = jnp.exp2(s_buf[step - low] - peak)
            s_buf[step - low] = expos
            part = tot[...]
            for lane in range(0, chunk, 128):
                part = part + expos[:, lane : lane + 128]
            tot[...] = part
            out[...] += jnp.dot(
                expos.astype(jnp.bfloat16),
                v_all[row, pl.ds(start, chunk), :],
                preferred_element_type=jnp.float32,
            )

        grads = g_all[tile, :block, :]
        total = jnp.sum(tot[...], axis=1, keepdims=True)
        attended = (out[...] / total).astype(jnp.bfloat16)
        att_ref[tile] = attended
        delta = jnp.sum(
            grads.astype(jnp.float32) * attended.astype(jnp.float32), axis=1, keepdims=True
        )
        lanes = lax.broadcasted_iota(jnp.int32, (block, 128), 1)
        columns = jnp.where(lanes == 0, peak + jnp.log2(total), delta)
        span = st_own.shape[-1]
        columns = jnp.concatenate([columns, jnp.zeros((span - block, 128), jnp.float32)], axis=0)
        st_own[tile] = columns.T[:8]

        @pl.loop(low, high)
        def _(step):
            row = step // per
            start = pl.multiple_of((step % per) * chunk, chunk)
            dprob = dot_nt(grads, v_all[row, pl.ds(start, chunk), :])
            dscore = (s_buf[step - low] * (dprob - delta)).astype(jnp.bfloat16)
            grad[...] += jnp.dot(
                dscore, k_all[row, pl.ds(start, chunk), :], preferred_element_type=jnp.float32
            )

        gq_ref[tile] = (grad[...] * (scale / total)).astype(jnp.bfloat16)

    swap_att().start()
    send_direct(4, st_own)
    first = lax.broadcasted_iota(jnp.int32, (tiles, 8, wide), 1) == 0
    stats_ref[...] = jnp.where(first, FAR, 0.0)
    stats_ref[:, :, :block] = st_own[:, :, :block]
    receive(4, (1, 2))
    send_onward(4)
    for which in (2, 3, 4):
        receive(which, (3, 4, 5, 6, 7, 8))
    for slot in range(1, 9):
        @pl.when(exists[slot])
        def _():
            stats_ref[:, :, slot * block : (slot + 1) * block] = st_all[slot, :, :, :block]
    for which, source in enumerate((k_ref, v_ref, q_ref, slot_of(3, 0), st_own)):
        sent(which, source)
    swap_att().wait()
    other_ref[...] = att_in[...]


def key_kernel(
    k_ref, v_ref, live_ref, stats_ref, q_all, g_all, gw_ref,
    gk_ref, gv_ref, share_ref,
    grad_k, grad_v, in_w, in_t, sum_w, send_t, w_send, w_recv, t_send, t_recv,
    *, tiles, block, wide, chunk, scale,
):
    per = wide // chunk
    t_index, w_index, h_index = (lax.axis_index(name) for name in ("tm", "width", "head"))
    t_count, w_count = lax.axis_size("tm"), lax.axis_size("width")

    def w_copy(hop):
        dest = lax.rem(w_index + hop, w_count)
        return pltpu.make_async_remote_copy(
            src_ref=gw_ref.at[:, dest], dst_ref=in_w.at[hop - 1],
            send_sem=w_send.at[hop - 1], recv_sem=w_recv.at[hop - 1],
            device_id=(t_index, dest, h_index), device_id_type=MESH,
        )

    def t_copy(hop):
        dest = lax.rem(t_index + hop, t_count)
        return pltpu.make_async_remote_copy(
            src_ref=send_t.at[dest], dst_ref=in_t.at[hop - 1],
            send_sem=t_send.at[hop - 1], recv_sem=t_recv.at[hop - 1],
            device_id=(dest, w_index, h_index), device_id_type=MESH,
        )

    barrier = pltpu.get_barrier_semaphore()
    for hop in range(1, w_count):
        pl.semaphore_signal(
            barrier, inc=1, device_id=(t_index, lax.rem(w_index + hop, w_count), h_index),
            device_id_type=MESH,
        )
    for hop in range(1, t_count):
        pl.semaphore_signal(
            barrier, inc=1, device_id=(lax.rem(t_index + hop, t_count), w_index, h_index),
            device_id_type=MESH,
        )
    pl.semaphore_wait(barrier, w_count + t_count - 2)
    for hop in range(1, w_count):
        w_copy(hop).start()

    @pl.loop(0, tiles)
    def _(tile):
        low = jnp.maximum(tile - 1, 0) * per
        high = (jnp.minimum(tile + 1, tiles - 1) + 1) * per
        @pl.when(tile == tiles // 2)
        def _():
            whole = gw_ref[:, w_index].astype(jnp.float32)
            for hop in range(1, w_count):
                w_copy(hop).wait()
                whole = whole + in_w[hop - 1].astype(jnp.float32)
            sum_w[...] = whole
            send_t[...] = whole.astype(jnp.bfloat16)
            for hop in range(1, t_count):
                t_copy(hop).start()

        grad_k[...] = jnp.zeros(grad_k.shape, jnp.float32)
        grad_v[...] = jnp.zeros(grad_v.shape, jnp.float32)

        @pl.loop(low, high)
        def _(step):
            row = step // per
            start = pl.multiple_of((step % per) * chunk, chunk)
            queries = q_all[row, pl.ds(start, chunk), :]
            grads = g_all[row, pl.ds(start, chunk), :]
            lse = stats_ref[row, 0:1, pl.ds(start, chunk)]
            delta = stats_ref[row, 1:2, pl.ds(start, chunk)]
            probs = jnp.exp2(dot_nt(k_ref[tile], queries) * (scale * LOG2E) - lse)
            grad_v[...] += jnp.dot(
                probs.astype(jnp.bfloat16), grads, preferred_element_type=jnp.float32
            )
            dscore = probs * (dot_nt(v_ref[tile], grads) - delta)
            grad_k[...] += jnp.dot(
                dscore.astype(jnp.bfloat16), queries, preferred_element_type=jnp.float32
            )

        live = live_ref[tile] > 0
        gk_ref[tile] = jnp.where(live, grad_k[...] * scale, 0.0).astype(jnp.bfloat16)
        gv_ref[tile] = jnp.where(live, grad_v[...], 0.0).astype(jnp.bfloat16)

    share = sum_w[t_index]
    for hop in range(1, t_count):
        t_copy(hop).wait()
        share = share + in_t[hop - 1].astype(jnp.float32)
    share_ref[...] = share


def lay_out(cells, block, tile_rows):
    frames, columns, rows, depth = cells.shape
    tiles = rows // tile_rows
    cells = cells.reshape(frames * columns, tiles, tile_rows, depth).transpose(1, 0, 2, 3)
    cells = cells.reshape(tiles, frames * columns * tile_rows, depth)
    return jnp.pad(cells, ((0, 0), (0, block - cells.shape[1]), (0, 0)))


def lay_back(cells, frames, columns, tile_rows):
    tiles, _, depth = cells.shape
    count = frames * columns
    cells = cells[:, : count * tile_rows].reshape(tiles, count, tile_rows, depth)
    return cells.transpose(1, 0, 2, 3).reshape(frames, columns, tiles * tile_rows, depth)


def shards(query_heads, key_heads, value_heads, row_valid, out_weight, grad_mixed):
    frames, rows, columns, depth = query_heads.shape
    scale = 1.0 / math.sqrt(depth)
    tiles = rows // TH
    count = frames * columns * TH
    block = round_up(count, 16)
    wide = round_up(9 * block, 256)
    chunk = wide // 2
    swap = (0, 2, 1, 3)
    query = lay_out(query_heads.transpose(swap), block, TH)
    key = lay_out(key_heads.transpose(swap), block, TH)
    value = lay_out(value_heads.transpose(swap), block, TH)
    grad_in = grad_mixed.transpose(swap)

    t_index, w_index = lax.axis_index("tm"), lax.axis_index("width")
    t_back, t_ahead = t_index > 0, t_index < lax.axis_size("tm") - 1
    w_back, w_ahead = w_index > 0, w_index < lax.axis_size("width") - 1
    exists = jnp.stack([
        t_index >= 0, t_back, t_ahead, w_back, w_ahead,
        t_back & w_back, t_ahead & w_back, t_back & w_ahead, t_ahead & w_ahead,
    ])
    live = jnp.broadcast_to(
        (row_valid > 0).reshape(tiles, 1, TH), (tiles, frames * columns, TH)
    ).reshape(tiles, count)
    live = jnp.pad(live, ((0, 0), (0, block - count)))
    wide_live = (live[:, None, :] & exists[None, :, None]).reshape(tiles, 9 * block)
    wide_live = jnp.pad(wide_live, ((0, 0), (0, wide - 9 * block)))
    bias = jnp.where(wide_live, 0.0, -FAR).astype(jnp.float32)[:, None, :]

    grad_heads = lax.dot_general(
        grad_in, out_weight, (((3,), (1,)), ((), ())), preferred_element_type=jnp.float32
    )
    parts = lay_out(grad_heads.astype(jnp.bfloat16), block, TH)
    low_part, high_part = parts[..., :depth], parts[..., depth:]
    first = lax.axis_index("head") == 0
    part_own = jnp.where(first, low_part, high_part)
    part_other = jnp.where(first, high_part, low_part)

    pairs = tiles * 3 - 2
    work = pairs * block * wide
    in_vmem = pl.BlockSpec(memory_space=pltpu.VMEM)
    params = dict(tiles=tiles, block=block, wide=wide, chunk=chunk, scale=scale)
    flat = jax.ShapeDtypeStruct((tiles, block, depth), jnp.bfloat16)
    wide_bf16 = pltpu.VMEM((tiles, wide, depth), jnp.bfloat16)
    acc = pltpu.VMEM((block, depth), jnp.float32)
    lane_acc = pltpu.VMEM((block, 128), jnp.float32)
    cost = pl.CostEstimate(
        flops=16 * work * depth, transcendentals=work, bytes_accessed=4 * tiles * wide * depth
    )
    spread = jax.ShapeDtypeStruct((tiles, wide, depth), jnp.bfloat16)
    span = round_up(block, 128)
    tile_bf16 = pltpu.VMEM((tiles, block, depth), jnp.bfloat16)
    attended, other, grad_query, query_wide, grad_wide, stats_wide = pl.pallas_call(
        functools.partial(query_kernel, **params),
        out_shape=(
            flat, flat, flat, spread, spread,
            jax.ShapeDtypeStruct((tiles, 8, wide), jnp.float32),
        ),
        in_specs=[in_vmem] * 6,
        out_specs=(in_vmem,) * 6,
        scratch_shapes=[
            wide_bf16, wide_bf16,
            pltpu.VMEM((min(3, tiles) * (wide // chunk), block, chunk), jnp.float32),
            lane_acc, lane_acc, acc, acc, tile_bf16, tile_bf16,
            pltpu.VMEM((tiles, 8, span), jnp.float32),
            pltpu.VMEM((9, tiles, 8, span), jnp.float32),
            pltpu.SemaphoreType.DMA((5, 9)),
            pltpu.SemaphoreType.DMA((5, 9)),
            pltpu.SemaphoreType.DMA((3,)),
            pltpu.SemaphoreType.DMA((2,)),
            pltpu.SemaphoreType.DMA((2,)),
        ],
        compiler_params=pltpu.CompilerParams(
            vmem_limit_bytes=56 << 20, collective_id=0, has_side_effects=True
        ),
        cost_estimate=cost,
        name="query_side",
    )(key, value, query, part_own, part_other, bias)

    attended = lay_back(attended, frames, columns, TH)
    other = lay_back(other, frames, columns, TH)
    heads_all = jnp.concatenate(
        [jnp.where(first, attended, other), jnp.where(first, other, attended)], axis=3
    )
    mixed = lax.dot_general(
        heads_all, out_weight, (((3,), (0,)), ((), ())), preferred_element_type=jnp.float32
    ).astype(jnp.bfloat16)
    t_count, w_count = lax.axis_size("tm"), lax.axis_size("width")
    share_rows, width = out_weight.shape[0] // (t_count * w_count), out_weight.shape[1]
    terms = lax.dot_general(
        heads_all, grad_in, (((0, 1, 2), (0, 1, 2)), ((), ())),
        preferred_element_type=jnp.float32,
    ).astype(jnp.bfloat16).reshape(t_count, w_count, share_rows, width)

    live_rows = live.astype(jnp.float32)[:, :, None]
    grad_key, grad_value, grad_weight = pl.pallas_call(
        functools.partial(key_kernel, **params),
        out_shape=(flat, flat, jax.ShapeDtypeStruct((share_rows, width), jnp.float32)),
        in_specs=[in_vmem] * 7,
        out_specs=(in_vmem,) * 3,
        scratch_shapes=[
            acc, acc,
            pltpu.VMEM((w_count - 1, t_count, share_rows, width), jnp.bfloat16),
            pltpu.VMEM((t_count - 1, share_rows, width), jnp.bfloat16),
            pltpu.VMEM((t_count, share_rows, width), jnp.float32),
            pltpu.VMEM((t_count, share_rows, width), jnp.bfloat16),
            pltpu.SemaphoreType.DMA((w_count - 1,)),
            pltpu.SemaphoreType.DMA((w_count - 1,)),
            pltpu.SemaphoreType.DMA((t_count - 1,)),
            pltpu.SemaphoreType.DMA((t_count - 1,)),
        ],
        compiler_params=pltpu.CompilerParams(
            vmem_limit_bytes=50 << 20, collective_id=1, has_side_effects=True
        ),
        cost_estimate=cost,
        name="key_side",
    )(key, value, live_rows, stats_wide, query_wide, grad_wide, terms)

    back = lambda cells: lay_back(cells, frames, columns, TH).transpose(swap)
    return (mixed.transpose(swap), back(grad_query), back(grad_key), back(grad_value), grad_weight)


def solution(mesh):
    split = P("tm", None, "width", "head")
    return jax.shard_map(
        shards,
        mesh=mesh,
        in_specs=(split, split, split, P(), P(None, "head"), split),
        out_specs=(split, split, split, split, P(("tm", "width"), "head")),
        check_vma=False,
    )
```
